32 devices in a mesh: ctx: 8 (over y, x, core), head: 4 (over z).
Axes of the slice: x: 2, y: 2, z: 4, core: 2. Of those that a mesh axis runs over, the one named last changes fastest.
Arguments:
- tokens_x: bfloat16 [4096, 8192], P('ctx', 'head'), may hold values from -121 to 121
- raw_dt: float32 [128, 4096], P('head', 'ctx'), may hold values from -4 to 4
- in_b: bfloat16 [4096, 128], P('ctx'), may hold values from -0.5 to 0.5
- in_c: bfloat16 [4096, 128], P('ctx'), may hold values from -0.5 to 0.5
- decay_rate: float32 [128], P('head'), may hold values from 4.8828125e-06 to 2
- skip_gain: float32 [128], P('head'), may hold values from 0.5 to 1.5
- step_bias: float32 [128], P('head'), may hold values from -5 to -3
- grad_y: bfloat16 [4096, 8192], P('ctx', 'head'), may hold values from -121 to 121
Outputs:
- grad_x: bfloat16 [4096, 8192], P('ctx', 'head')
- grad_raw_dt: float32 [128, 4096], P('head', 'ctx')
- grad_b: float32 [4096, 128], P('ctx')
- grad_c: float32 [4096, 128], P('ctx')
- grad_rate: float32 [128], P('head')
- grad_skip: float32 [128], P('head')
- grad_bias: float32 [128], P('head')
The draws below stay inside these ranges and needn't reach their ends.
All inputs are finite; a program needn't handle non-finite values.
Results may differ from the reference program's by a relative error of at most 0.001.
Values sent between devices are 32-bit elements; how exact they have to be, the bound alone decides.
A program may use at most 128 MiB of HBM per device.

```python
import math
import jax
import jax.numpy as jnp
from jax import lax

HEADS = 128
HEAD_DIM = 64
STATE = 128
BLOCK = 256
TOK_DEV = 512
TOKENS = 4096


rise_level = 3.0


def head_kinds(key):
    kind_pick = jax.random.randint(jax.random.fold_in(key, 101), (HEADS,), 0, 8)
    balanced = kind_pick < 2
    quiet_heads = (kind_pick >= 2) & (kind_pick < 5)
    return (balanced, quiet_heads)


def bias_values(key):
    return jax.random.uniform(jax.random.fold_in(key, 102), (HEADS,), jnp.float32, -5.0, -3.0)


def column_spread(key, direction):
    balanced, quiet_heads = head_kinds(key)
    position = jnp.arange(TOKENS, dtype=jnp.float32) / max(TOKENS - 1, 1)
    level_curve = jnp.exp(direction * rise_level * (1.0 - 2.0 * position))
    column_scale = jnp.where(balanced[None, :], level_curve[:, None], 1.0)
    return jnp.repeat(column_scale, HEAD_DIM, axis=1)


def noise_field(noise_key):
    array_shape = (TOKENS, HEADS * HEAD_DIM)
    noise_values = jnp.clip(jax.random.normal(noise_key, array_shape, jnp.float32), -6.0, 6.0)
    return noise_values


def draw_tokens_x(key, part):
    return (noise_field(jax.random.fold_in(key, 105)) * column_spread(key, 1.0)).astype(jnp.bfloat16)


def draw_grad_y(key, part):
    return (noise_field(jax.random.fold_in(key, 106)) * column_spread(key, -1.0)).astype(jnp.bfloat16)


def draw_step_bias(key, part):
    return bias_values(key)


def draw_decay_rate(key, part):
    balanced, quiet_heads = head_kinds(key)
    head_bias = bias_values(key)
    pieces = TOKENS // TOK_DEV
    mean_step = TOK_DEV * jnp.exp(head_bias + 0.5)
    draw_keys = jax.random.split(jax.random.fold_in(key, 103), 3)
    drawn_rate = jnp.exp(jax.random.uniform(draw_keys[0], (HEADS,), jnp.float32, math.log(1.0 / (50 * TOKENS)), math.log(1.5)))
    growth = 2.0 * rise_level / max(pieces - 1, 1)
    balanced_rate = jax.random.uniform(draw_keys[1], (HEADS,), jnp.float32, 1.3, 1.7) * growth / mean_step
    quiet_rate = jnp.exp(jax.random.uniform(draw_keys[2], (HEADS,), jnp.float32, math.log(0.7), math.log(2.5))) / mean_step
    return jnp.where(balanced, balanced_rate, jnp.where(quiet_heads, quiet_rate, drawn_rate))


def draw_raw_dt(key, part):
    balanced, quiet_heads = head_kinds(key)
    draw_keys = jax.random.split(jax.random.fold_in(key, 104), 4)
    outside = jnp.clip(jax.random.normal(draw_keys[0], (HEADS, TOKENS), jnp.float32), -4.0, 4.0)
    inside = jax.random.uniform(draw_keys[1], (HEADS, TOKENS), jnp.float32, -4.0, -2.5)
    gap_start = jax.random.uniform(draw_keys[2], (HEADS, 1), jnp.float32, 0.1, 0.3) * TOKENS
    gap_end = jax.random.uniform(draw_keys[3], (HEADS, 1), jnp.float32, 0.7, 0.9) * TOKENS
    position = jnp.arange(TOKENS, dtype=jnp.float32)[None, :]
    in_gap = quiet_heads[:, None] & (position >= gap_start) & (position < gap_end)
    return jnp.where(in_gap, inside, outside)


def shard_levels(own_key, dims, cuts, least, high):
    level = 1.0
    for dim, parts in cuts:
        heights = jax.random.uniform(jax.random.fold_in(jax.random.fold_in(own_key, 6), dim), (parts,), jnp.float32, least / len(cuts), high / len(cuts))
        level = level * jnp.repeat(jnp.exp(heights), dims[dim] // parts).reshape((-1,) + (1,) * (len(dims) - 1 - dim))
    return level


def centred(key, shape, deviation, reach, shards=(), kind=jnp.bfloat16):
    entries = deviation * jax.random.normal(key, shape, jnp.float32)
    if shards:
        entries = entries * shard_levels(key, shape, shards, -0.22, 0.18)
    return jnp.clip(entries, -reach, reach).astype(kind)


def setup_inputs(seed: int = 0) -> dict:
    seeds = jax.random.split(jax.random.key(seed), 9)
    tokens_x = draw_tokens_x(jax.random.fold_in(seeds[8], 71), 0)
    raw_dt = draw_raw_dt(jax.random.fold_in(seeds[8], 71), 0)
    in_b = centred(seeds[2], (TOKENS, STATE), STATE ** -0.5, 0.5, ((0, 8),))
    in_c = centred(seeds[3], (TOKENS, STATE), STATE ** -0.5, 0.5, ((0, 8),))
    decay_rate = draw_decay_rate(jax.random.fold_in(seeds[8], 71), 0)
    skip_gain = jnp.clip(0.5 + 1.0 * jax.random.uniform(seeds[5], (HEADS,), jnp.float32) ** shard_levels(seeds[5], (HEADS,), ((0, 4),), -0.2, 0.2), 0.5, 1.5)
    step_bias = draw_step_bias(jax.random.fold_in(seeds[8], 71), 0)
    grad_y = draw_grad_y(jax.random.fold_in(seeds[8], 71), 0)
    return dict(tokens_x=tokens_x, raw_dt=raw_dt, in_b=in_b, in_c=in_c, decay_rate=decay_rate, skip_gain=skip_gain, step_bias=step_bias, grad_y=grad_y)


def layer_forward(values, raw_dt, in_b, in_c, decay_rate, skip_gain, step_bias, start_state):
    token_count, head_count, head_size = values.shape
    state_size = in_b.shape[1]
    block_count = token_count // BLOCK
    step_sizes = jax.nn.softplus(raw_dt + step_bias[:, None])
    log_decay = -decay_rate[:, None] * step_sizes
    x_blocks = values.reshape(block_count, BLOCK, head_count, head_size)
    step_blocks = step_sizes.reshape(head_count, block_count, BLOCK).transpose(1, 0, 2)
    decay_blocks = log_decay.reshape(head_count, block_count, BLOCK).transpose(1, 0, 2)
    b_blocks = in_b.reshape(block_count, BLOCK, state_size)
    c_blocks = in_c.reshape(block_count, BLOCK, state_size)
    positions = jnp.arange(BLOCK)
    causal = positions[:, None] >= positions[None, :]

    def one_block(carry_state, pieces):
        x_block, step_block, decay_block, b_block, c_block = pieces
        cum_decay = jnp.cumsum(decay_block, axis=1)
        scores = jnp.dot(c_block, b_block.T, precision=lax.Precision.HIGHEST)
        log_gap = cum_decay[:, :, None] - cum_decay[:, None, :]
        mixing = jnp.where(causal[None], jnp.exp(jnp.where(causal[None], log_gap, 0.0)), 0.0)
        mixing = mixing * scores[None] * step_block[:, None, :]
        within = jnp.einsum('hts,shp->thp', mixing, x_block, precision=lax.Precision.HIGHEST)
        carried = jnp.einsum('hpn,tn->thp', carry_state, c_block, precision=lax.Precision.HIGHEST)
        carried = carried * jnp.exp(cum_decay).T[:, :, None]
        block_out = within + carried + skip_gain[None, :, None] * x_block
        end_decay = cum_decay[:, -1]
        state_weight = jnp.exp(end_decay[:, None] - cum_decay) * step_block
        weighted = x_block * state_weight.T[:, :, None]
        next_state = jnp.exp(end_decay)[:, None, None] * carry_state
        next_state = next_state + jnp.einsum('shp,sn->hpn', weighted, b_block, precision=lax.Precision.HIGHEST)
        return (next_state, block_out)
    final_state, block_outs = lax.scan(jax.checkpoint(one_block), start_state, (x_blocks, step_blocks, decay_blocks, b_blocks, c_blocks))
    return (block_outs.reshape(token_count, head_count, head_size), final_state)

def reference(tokens_x, raw_dt, in_b, in_c, decay_rate, skip_gain, step_bias, grad_y):
    values = tokens_x.astype(jnp.float32).reshape(TOKENS, HEADS, HEAD_DIM)
    b_full = in_b.astype(jnp.float32)
    c_full = in_c.astype(jnp.float32)
    cotangent = grad_y.astype(jnp.float32).reshape(TOKENS, HEADS, HEAD_DIM)
    start_state = jnp.zeros((HEADS, HEAD_DIM, STATE), jnp.float32)

    def forward(values, raw_dt, b_full, c_full, decay_rate, skip_gain, step_bias):
        outputs, final_state = layer_forward(values, raw_dt, b_full, c_full, decay_rate, skip_gain, step_bias, start_state)
        return outputs
    outputs, pullback = jax.vjp(forward, values, raw_dt, b_full, c_full, decay_rate, skip_gain, step_bias)
    grad_v, grad_raw, grad_b, grad_c, grad_rate, grad_skip, grad_bias = pullback(cotangent)
    grad_x = grad_v.reshape(TOKENS, HEADS * HEAD_DIM).astype(jnp.bfloat16)
    return (grad_x, grad_raw, grad_b, grad_c, grad_rate, grad_skip, grad_bias)
```

```python
import jax
import jax.numpy as jnp
from jax import lax
from jax.experimental import pallas as pl
from jax.experimental.pallas import tpu as pltpu
from jax.sharding import PartitionSpec as P

CHUNK = 128
GROUP = 8
F32 = jnp.float32
BF16 = jnp.bfloat16
HIGH = lax.Precision.HIGHEST
NT = (((1,), (1,)), ((), ()))
PARAMS = pltpu.CompilerParams(vmem_limit_bytes=56 << 20)


def mm(a, b):
    return jnp.dot(a, b, preferred_element_type=F32)


def mm_nt(a, b):
    return lax.dot_general(a, b, NT, preferred_element_type=F32)


def split(a):
    high = a.astype(BF16)
    return high, (a - high.astype(F32)).astype(BF16)


def softplus(v):
    return jnp.maximum(v, 0.0) + jnp.log1p(jnp.exp(-jnp.abs(v)))


def step_sizes(raw_ref, bias_ref):
    return softplus(raw_ref[...] + bias_ref[...])


def lanes(column, width=CHUNK):
    return jnp.broadcast_to(column, (column.shape[0], width))


def per_head(rows, matrix):
    heads = rows.shape[0]
    shaped = matrix.reshape(heads, matrix.shape[0] // heads, matrix.shape[1])
    return (shaped * rows[:, None, :]).reshape(matrix.shape)


def head_sums(matrix, heads):
    return jnp.sum(matrix.reshape(heads, matrix.shape[0] // heads, matrix.shape[1]), axis=1)


def pair_blocks(first, second):
    zero = jnp.zeros_like(first)
    return jnp.concatenate(
        [jnp.concatenate([first, zero], axis=1), jnp.concatenate([zero, second], axis=1)], axis=0
    )


def triangle(lower):
    row = lax.broadcasted_iota(jnp.int32, (CHUNK, CHUNK), 0)
    col = lax.broadcasted_iota(jnp.int32, (CHUNK, CHUNK), 1)
    return (row >= col) if lower else (row <= col)


def span_of(c):
    return slice(c * CHUNK, (c + 1) * CHUNK)


def states_kernel(x_ref, g_ref, raw_ref, bias_ref, rate_ref, b_ref, c_ref,
                  xt_ref, gt_ref, dt_ref, cum_ref, end_ref, s_ref, r_ref):
    heads, tokens = raw_ref.shape
    chunks = tokens // CHUNK
    dt = step_sizes(raw_ref, bias_ref)
    dt_ref[...] = dt
    log_decay = -rate_ref[...] * dt
    ones = triangle(False).astype(F32)
    xt_ref[...] = x_ref[...].T
    gt_ref[...] = g_ref[...].T
    cums = [jnp.dot(log_decay[:, span_of(c)], ones, precision=HIGH) for c in range(chunks)]
    ends = [lanes(cum[:, CHUNK - 1:]) for cum in cums]
    total = ends[0]
    for end in ends[1:]:
        total = total + end
    end_ref[...] = total
    state = None
    for c in range(chunks):
        cum_ref[:, span_of(c)] = cums[c]
        weight = jnp.exp(ends[c] - cums[c]) * dt[:, span_of(c)]
        high, low = split(per_head(weight, xt_ref[:, span_of(c)].astype(F32)))
        b = b_ref[span_of(c), :]
        added = mm(high, b) + mm(low, b)
        state = added if state is None else per_head(jnp.exp(ends[c]), state) + added
        s_ref[c] = state
    back = None
    for c in reversed(range(chunks)):
        high, low = split(per_head(jnp.exp(cums[c]), gt_ref[:, span_of(c)].astype(F32)))
        cc = c_ref[span_of(c), :]
        added = mm(high, cc) + mm(low, cc)
        back = added if back is None else per_head(jnp.exp(ends[c]), back) + added
        r_ref[c] = back


def within_kernel(x_ref, xt_ref, gt_ref, dt_ref, cum_ref, b_ref, c_ref,
                  dxt_ref, row_ref, col_ref, dg_ref):
    heads, tokens = dt_ref.shape
    size = xt_ref.shape[0] // heads
    group = pl.program_id(0)
    causal = triangle(False)

    @pl.when(group == 0)
    def _():
        dg_ref[...] = jnp.zeros_like(dg_ref)

    def one_chunk(c, carry):
        at = pl.ds(pl.multiple_of(c * CHUNK, CHUNK), CHUNK)
        scores = mm_nt(b_ref[at, :], c_ref[at, :])
        cum = cum_ref[:, at]
        shifted = (cum - jnp.log(dt_ref[:, at])).T
        total = jnp.zeros((CHUNK, CHUNK), F32)
        rows, cols = [], []
        for pair in range(heads // 2):
            x_pair = x_ref[at, pair * 2 * size:(pair + 1) * 2 * size]
            places = [slice((2 * pair + j) * size, (2 * pair + j + 1) * size) for j in range(2)]
            products = mm(x_pair, pair_blocks(gt_ref[places[0], at], gt_ref[places[1], at]))
            for j in range(2):
                h = 2 * pair + j
                gap = cum[h:h + 1, :] - shifted[:, h:h + 1]
                decay = jnp.exp(jnp.where(causal, gap, -1e30))
                total = total + products[:, j * CHUNK:(j + 1) * CHUNK] * decay
                high, low = split(decay * scores)
                x_h = xt_ref[places[j], at]
                g_h = gt_ref[places[j], at]
                y_h = mm(x_h, high) + mm(x_h, low)
                dx_h = mm_nt(g_h, high) + mm_nt(g_h, low)
                dxt_ref[places[j], at] = dx_h
                rows.append(jnp.sum(y_h * g_h.astype(F32), axis=0, keepdims=True))
                cols.append(jnp.sum(dx_h * x_h.astype(F32), axis=0, keepdims=True))
        row_ref[:, at] = jnp.concatenate(rows, axis=0)
        col_ref[:, at] = jnp.concatenate(cols, axis=0)
        dg_ref[c] += total
        return carry

    lax.fori_loop(0, tokens // CHUNK, one_chunk, 0)


def across_kernel(x_ref, g_ref, xt_ref, gt_ref, raw_ref, bias_ref, rate_ref, skip_ref, dt_ref,
                  cum_ref, s_ref, r_ref, sin_ref, rin_ref, dxt_ref, row_ref, col_ref,
                  b_ref, c_ref, dg_ref,
                  gx_ref, graw_ref, gparam_ref, db_ref, dc_ref):
    heads, tokens = dt_ref.shape
    chunks = tokens // CHUNK
    size = xt_ref.shape[0] // heads
    group = pl.program_id(0)

    @pl.when(group == 0)
    def _():
        for c in range(chunks):
            high, low = split(dg_ref[c])
            db_ref[span_of(c), :] = mm(high, c_ref[span_of(c), :]) + mm(low, c_ref[span_of(c), :])
            high, low = split(dg_ref[c].T)
            dc_ref[span_of(c), :] = mm(high, b_ref[span_of(c), :]) + mm(low, b_ref[span_of(c), :])

    ends = [lanes(cum_ref[:, (c + 1) * CHUNK - 1:(c + 1) * CHUNK]) for c in range(chunks)]
    before = [jnp.zeros_like(ends[0])]
    for end in ends:
        before.append(before[-1] + end)
    after = [jnp.zeros_like(ends[0])]
    for end in reversed(ends):
        after.insert(0, after[0] + end)
    skip = lanes(skip_ref[...])
    rate = lanes(rate_ref[...])
    rows, cols, crossed = [], [], None
    for c in range(chunks):
        at = span_of(c)
        cum, dt = cum_ref[:, at], dt_ref[:, at]
        reach = jnp.exp(cum)
        weight = jnp.exp(ends[c] - cum) * dt
        state = per_head(jnp.exp(before[c]), sin_ref[...])
        if c > 0:
            state = state + s_ref[c - 1]
        back = per_head(jnp.exp(after[c + 1]), rin_ref[...])
        if c < chunks - 1:
            back = back + r_ref[c + 1]
        s_high, s_low = split(state)
        r_high, r_low = split(back)
        b, cc = b_ref[at, :], c_ref[at, :]
        xt, gt = xt_ref[:, at].astype(F32), gt_ref[:, at].astype(F32)
        y = mm_nt(s_high, cc) + mm_nt(s_low, cc)
        rows.append(row_ref[:, at] + head_sums(y * gt, heads) * reach)
        dx = per_head(weight, mm_nt(r_high, b) + mm_nt(r_low, b))
        cols.append(col_ref[:, at] + head_sums(dx * xt, heads))
        product = head_sums(xt * gt, heads)
        crossed = product if crossed is None else crossed + product
        dx = dx + dxt_ref[:, at] + per_head(skip, gt)
        gx_ref[at, :] = dx.astype(BF16).T
        reach_t, weight_t = reach.T, weight.T
        dc = jnp.zeros((CHUNK, cc.shape[1]), F32)
        db = jnp.zeros((CHUNK, cc.shape[1]), F32)
        width = cc.shape[1]
        for pair in range(heads // 2):
            wide = slice(pair * 2 * size, (pair + 1) * 2 * size)
            one = slice(2 * pair * size, (2 * pair + 1) * size)
            two = slice((2 * pair + 1) * size, (2 * pair + 2) * size)
            g_pair, x_pair = g_ref[at, wide], x_ref[at, wide]
            gs = (mm(g_pair, pair_blocks(s_high[one], s_high[two]))
                  + mm(g_pair, pair_blocks(s_low[one], s_low[two])))
            xr = (mm(x_pair, pair_blocks(r_high[one], r_high[two]))
                  + mm(x_pair, pair_blocks(r_low[one], r_low[two])))
            for j in range(2):
                h = 2 * pair + j
                dc = dc + gs[:, j * width:(j + 1) * width] * reach_t[:, h:h + 1]
                db = db + xr[:, j * width:(j + 1) * width] * weight_t[:, h:h + 1]
        dc_ref[at, :] += dc
        db_ref[at, :] += db
    last = s_ref[chunks - 1] + per_head(jnp.exp(before[chunks]), sin_ref[...])
    beyond = lanes(jnp.sum(head_sums(last * rin_ref[...], heads), axis=1, keepdims=True))
    suffix = triangle(True).astype(F32)
    g_rate = jnp.zeros((heads, 1), F32)
    g_bias = jnp.zeros((heads, 1), F32)
    for c in reversed(range(chunks)):
        at = span_of(c)
        change = rows[c] - cols[c]
        d_log = jnp.dot(change, suffix, precision=HIGH) + beyond
        beyond = beyond + lanes(jnp.sum(change, axis=1, keepdims=True))
        dt = dt_ref[:, at]
        g_dt = cols[c] / dt - rate * d_log
        v = raw_ref[:, at] + bias_ref[...]
        g_raw = g_dt / (1.0 + jnp.exp(-v))
        graw_ref[:, at] = g_raw
        g_rate = g_rate - jnp.sum(dt * d_log, axis=1, keepdims=True)
        g_bias = g_bias + jnp.sum(g_raw, axis=1, keepdims=True)
    g_skip = jnp.sum(crossed, axis=1, keepdims=True)
    lane = lax.broadcasted_iota(jnp.int32, (heads, CHUNK), 1)
    gparam_ref[...] = jnp.where(lane == 0, g_rate, jnp.where(lane == 1, g_skip, g_bias))


def hypercube_shift(value, axis, distance):
    peers = lax.axis_size(axis)
    return lax.ppermute(value, axis, [(i, i ^ distance) for i in range(peers)])


def carried(span, states, adjoints, axis):
    peers, place = lax.axis_size(axis), lax.axis_index(axis)
    heads = span.shape[0]
    half = heads // 2
    odd = (place % 2) == 1

    def halves(whole):
        first, second = whole[:half], whole[half:]
        return jnp.where(odd, second, first), jnp.where(odd, first, second)

    def scale(log):
        return jnp.exp(log)[:, None, None]

    s_mine, s_theirs = halves(states)
    r_mine, r_theirs = halves(adjoints)
    other = hypercube_shift(span, axis, 1)
    s_got, r_got = hypercube_shift((s_theirs, r_theirs), axis, 1)
    log_mine, log_got = halves(span)[0], halves(other)[0]
    log_even, log_odd = jnp.where(odd, log_got, log_mine), jnp.where(odd, log_mine, log_got)
    s_even, s_odd = jnp.where(odd, s_got, s_mine), jnp.where(odd, s_mine, s_got)
    r_even, r_odd = jnp.where(odd, r_got, r_mine), jnp.where(odd, r_mine, r_got)
    s_all = scale(log_odd) * s_even + s_odd
    r_all = r_even + scale(log_even) * r_odd
    log_all = log_even + log_odd
    s_pre, r_pre = jnp.zeros_like(s_all), jnp.zeros_like(r_all)
    s_log, r_log = jnp.zeros_like(log_all), jnp.zeros_like(log_all)
    distance = 2
    while distance < peers:
        upper = (place // distance) % 2 == 1
        final = distance * 2 >= peers
        log_new = hypercube_shift(log_all, axis, distance)
        if final:
            s_new = r_new = hypercube_shift(jnp.where(upper, r_all, s_all), axis, distance)
        else:
            s_new, r_new = hypercube_shift((s_all, r_all), axis, distance)
        s_pre = jnp.where(upper, s_pre + scale(s_log) * s_new, s_pre)
        r_pre = jnp.where(upper, r_pre, r_pre + scale(r_log) * r_new)
        if not final:
            s_log = jnp.where(upper, s_log + log_new, s_log)
            r_log = jnp.where(upper, r_log, r_log + log_new)
            s_all = jnp.where(upper, scale(log_all) * s_new + s_all, scale(log_new) * s_all + s_new)
            r_all = jnp.where(upper, r_new + scale(log_new) * r_all, r_all + scale(log_all) * r_new)
            log_all = log_all + log_new
        distance *= 2
    s_for_odd = s_even + scale(log_even) * s_pre
    r_for_even = r_odd + scale(log_odd) * r_pre
    s_keep, s_give = jnp.where(odd, s_for_odd, s_pre), jnp.where(odd, s_pre, s_for_odd)
    r_keep, r_give = jnp.where(odd, r_pre, r_for_even), jnp.where(odd, r_for_even, r_pre)
    s_back, r_back = hypercube_shift((s_give, r_give), axis, 1)

    def whole(keep, back):
        return jnp.concatenate([jnp.where(odd, back, keep), jnp.where(odd, keep, back)], axis=0)

    return whole(s_keep, s_back), whole(r_keep, r_back)


def on_device(tokens_x, raw_dt, in_b, in_c, decay_rate, skip_gain, step_bias, grad_y):
    heads, tokens = raw_dt.shape
    width = tokens_x.shape[1]
    size = width // heads
    state = in_b.shape[1]
    chunks = tokens // CHUNK
    wide = GROUP * size
    grid = (heads // GROUP,)

    def shape(*dims, dtype=F32):
        return jax.ShapeDtypeStruct(dims, dtype)

    tokens_by_wide = pl.BlockSpec((tokens, wide), lambda i: (0, i))
    wide_by_tokens = pl.BlockSpec((wide, tokens), lambda i: (i, 0))
    head_rows = pl.BlockSpec((GROUP, tokens), lambda i: (i, 0))
    head_lanes = pl.BlockSpec((GROUP, CHUNK), lambda i: (i, 0))
    head_column = pl.BlockSpec((GROUP, 1), lambda i: (i, 0))
    projection = pl.BlockSpec((tokens, state), lambda i: (0, 0))
    state_block = pl.BlockSpec((wide, state), lambda i: (i, 0))
    state_blocks = pl.BlockSpec((chunks, wide, state), lambda i: (0, i, 0))
    score_blocks = pl.BlockSpec((chunks, CHUNK, CHUNK), lambda i: (0, 0, 0))
    bias, rate, skip = (v.reshape(heads, 1) for v in (step_bias, decay_rate, skip_gain))

    xt, gt, dt, cum, end, s_loc, r_loc = pl.pallas_call(
        states_kernel,
        grid=grid,
        in_specs=[tokens_by_wide, tokens_by_wide, head_rows, head_column, head_column,
                  projection, projection],
        out_specs=[wide_by_tokens, wide_by_tokens, head_rows, head_rows, head_lanes,
                   state_blocks, state_blocks],
        out_shape=[shape(width, tokens, dtype=BF16), shape(width, tokens, dtype=BF16),
                   shape(heads, tokens), shape(heads, tokens), shape(heads, CHUNK),
                   shape(chunks, width, state), shape(chunks, width, state)],
        compiler_params=PARAMS,
        name="states",
    )(tokens_x, grad_y, raw_dt, bias, rate, in_b, in_c)

    s_in, r_in = carried(
        end[:, 0],
        s_loc[chunks - 1].reshape(heads, size, state),
        r_loc[0].reshape(heads, size, state),
        "ctx",
    )

    dxt, row, col, dg = pl.pallas_call(
        within_kernel,
        grid=grid,
        in_specs=[tokens_by_wide, wide_by_tokens, wide_by_tokens, head_rows, head_rows,
                  projection, projection],
        out_specs=[wide_by_tokens, head_rows, head_rows, score_blocks],
        out_shape=[shape(width, tokens), shape(heads, tokens), shape(heads, tokens),
                   shape(chunks, CHUNK, CHUNK)],
        compiler_params=PARAMS,
        cost_estimate=pl.CostEstimate(
            flops=24 * width * tokens * CHUNK,
            bytes_accessed=14 * width * tokens,
            transcendentals=heads * tokens * CHUNK,
        ),
        name="within",
    )(tokens_x, xt, gt, dt, cum, in_b, in_c)

    grad_x, grad_raw, params, grad_b, grad_c = pl.pallas_call(
        across_kernel,
        grid=grid,
        in_specs=[tokens_by_wide, tokens_by_wide, wide_by_tokens, wide_by_tokens, head_rows,
                  head_column, head_column, head_column, head_rows, head_rows, state_blocks,
                  state_blocks, state_block, state_block, wide_by_tokens, head_rows, head_rows,
                  projection, projection, score_blocks],
        out_specs=[tokens_by_wide, head_rows, head_lanes, projection, projection],
        out_shape=[shape(tokens, width, dtype=BF16), shape(heads, tokens), shape(heads, CHUNK),
                   shape(tokens, state), shape(tokens, state)],
        compiler_params=PARAMS,
        name="across",
    )(tokens_x, grad_y, xt, gt, raw_dt, bias, rate, skip, dt, cum, s_loc, r_loc,
      s_in.reshape(width, state), r_in.reshape(width, state), dxt, row, col, in_b, in_c, dg)

    grad_b, grad_c = lax.psum((grad_b, grad_c), "head")
    params = params[:, :3]
    distance = 1
    while distance < lax.axis_size("ctx"):
        params = params + hypercube_shift(params, "ctx", distance)
        distance *= 2
    return (grad_x, grad_raw, grad_b, grad_c, params[:, 0], params[:, 1], params[:, 2])


def solution(mesh):
    placed = (
        P("ctx", "head"),
        P("head", "ctx"),
        P("ctx", None),
        P("ctx", None),
        P("head"),
        P("head"),
        P("head"),
        P("ctx", "head"),
    )
    return jax.shard_map(
        on_device,
        mesh=mesh,
        in_specs=placed,
        out_specs=(
            P("ctx", "head"),
            P("head", "ctx"),
            P("ctx", None),
            P("ctx", None),
            P("head"),
            P("head"),
            P("head"),
        ),
        check_vma=False,
    )
```

```python
import jax
import jax.numpy as jnp
from jax import lax
from jax.experimental import pallas as pl
from jax.experimental.pallas import tpu as pltpu
from jax.sharding import PartitionSpec as P


CHUNK = 128
GROUP = 8
F32 = jnp.float32
BF16 = jnp.bfloat16
HIGH = lax.Precision.HIGHEST
NT = (((1,), (1,)), ((), ()))
PARAMS = pltpu.CompilerParams(vmem_limit_bytes=56 << 20)


def mm(a, b):
    return jnp.dot(a, b, preferred_element_type=F32)


def mm_nt(a, b):
    return lax.dot_general(a, b, NT, preferred_element_type=F32)


def split(a):
    high = a.astype(BF16)
    return high, (a - high.astype(F32)).astype(BF16)


def softplus(v):
    return jnp.maximum(v, 0.0) + jnp.log1p(jnp.exp(-jnp.abs(v)))


def lanes(column, width=CHUNK):
    return jnp.broadcast_to(column, (column.shape[0], width))


def per_head(rows, matrix):
    heads = rows.shape[0]
    shaped = matrix.reshape(heads, matrix.shape[0] // heads, matrix.shape[1])
    return (shaped * rows[:, None, :]).reshape(matrix.shape)


def head_sums(matrix, heads):
    return jnp.sum(matrix.reshape(heads, matrix.shape[0] // heads, matrix.shape[1]), axis=1)


def pair_blocks(first, second):
    zero = jnp.zeros_like(first)
    return jnp.concatenate(
        [jnp.concatenate([first, zero], axis=1), jnp.concatenate([zero, second], axis=1)], axis=0
    )


def triangle(lower):
    row = lax.broadcasted_iota(jnp.int32, (CHUNK, CHUNK), 0)
    col = lax.broadcasted_iota(jnp.int32, (CHUNK, CHUNK), 1)
    return (row >= col) if lower else (row <= col)


def span_of(c):
    return slice(c * CHUNK, (c + 1) * CHUNK)


def states_kernel(x_ref, g_ref, raw_ref, knob_ref, b_ref, c_ref,
                  xt_ref, gt_ref, dt_ref, cum_ref, end_ref, s_ref, r_ref):
    _, tokens = raw_ref.shape
    chunks = tokens // CHUNK
    dt = softplus(raw_ref[...] + knob_ref[:, 0:1])
    dt_ref[...] = dt
    log_decay = -knob_ref[:, 1:2] * dt
    ones = triangle(False).astype(F32)
    xt_ref[...] = x_ref[...].T
    gt_ref[...] = g_ref[...].T
    cums = [jnp.dot(log_decay[:, span_of(c)], ones, precision=HIGH) for c in range(chunks)]
    ends = [lanes(cum[:, CHUNK - 1:]) for cum in cums]
    total = ends[0]
    for end in ends[1:]:
        total = total + end
    end_ref[...] = total
    state = None
    for c in range(chunks):
        cum_ref[:, span_of(c)] = cums[c]
        weight = jnp.exp(ends[c] - cums[c]) * dt[:, span_of(c)]
        high, low = split(per_head(weight, xt_ref[:, span_of(c)].astype(F32)))
        b = b_ref[span_of(c), :]
        added = mm(high, b) + mm(low, b)
        state = added if state is None else per_head(jnp.exp(ends[c]), state) + added
        s_ref[c] = state
    back = None
    for c in reversed(range(chunks)):
        high, low = split(per_head(jnp.exp(cums[c]), gt_ref[:, span_of(c)].astype(F32)))
        cc = c_ref[span_of(c), :]
        added = mm(high, cc) + mm(low, cc)
        back = added if back is None else per_head(jnp.exp(ends[c]), back) + added
        r_ref[c] = back


def within_kernel(x_ref, xt_ref, gt_ref, dt_ref, cum_ref, b_ref, c_ref,
                  dxt_ref, row_ref, col_ref, dg_ref):
    heads, tokens = dt_ref.shape
    size = xt_ref.shape[0] // heads
    group = pl.program_id(0)
    causal = triangle(False)

    @pl.when(group == 0)
    def _():
        dg_ref[...] = jnp.zeros_like(dg_ref)

    def one_chunk(c, carry):
        at = pl.ds(pl.multiple_of(c * CHUNK, CHUNK), CHUNK)
        scores = mm_nt(b_ref[at, :], c_ref[at, :])
        cum = cum_ref[:, at]
        shifted = (cum - jnp.log(dt_ref[:, at])).T
        total = jnp.zeros((CHUNK, CHUNK), F32)
        rows, cols = [], []
        for pair in range(heads // 2):
            x_pair = x_ref[at, pair * 2 * size:(pair + 1) * 2 * size]
            places = [slice((2 * pair + j) * size, (2 * pair + j + 1) * size) for j in range(2)]
            products = mm(x_pair, pair_blocks(gt_ref[places[0], at], gt_ref[places[1], at]))
            for j in range(2):
                h = 2 * pair + j
                gap = cum[h:h + 1, :] - shifted[:, h:h + 1]
                decay = jnp.exp(jnp.where(causal, gap, -1e30))
                total = total + products[:, j * CHUNK:(j + 1) * CHUNK] * decay
                high, low = split(decay * scores)
                x_h = xt_ref[places[j], at]
                g_h = gt_ref[places[j], at]
                y_h = mm(x_h, high) + mm(x_h, low)
                dx_h = mm_nt(g_h, high) + mm_nt(g_h, low)
                dxt_ref[places[j], at] = dx_h
                rows.append(jnp.sum(y_h * g_h.astype(F32), axis=0, keepdims=True))
                cols.append(jnp.sum(dx_h * x_h.astype(F32), axis=0, keepdims=True))
        row_ref[:, at] = jnp.concatenate(rows, axis=0)
        col_ref[:, at] = jnp.concatenate(cols, axis=0)
        dg_ref[c] += total
        return carry

    lax.fori_loop(0, tokens // CHUNK, one_chunk, 0)


def across_kernel(x_ref, g_ref, xt_ref, gt_ref, raw_ref, knob_ref, dt_ref, cum_ref,
                  s_ref, r_ref, sin_ref, rin_ref, dxt_ref, row_ref, col_ref,
                  b_ref, c_ref, dg_ref,
                  gx_ref, graw_ref, gparam_ref, dbc_ref):
    db_ref, dc_ref = dbc_ref.at[0], dbc_ref.at[1]
    heads, tokens = dt_ref.shape
    chunks = tokens // CHUNK
    size = xt_ref.shape[0] // heads
    group = pl.program_id(0)

    @pl.when(group == 0)
    def _():
        for c in range(chunks):
            high, low = split(dg_ref[c])
            db_ref[span_of(c), :] = mm(high, c_ref[span_of(c), :]) + mm(low, c_ref[span_of(c), :])
            high, low = split(dg_ref[c].T)
            dc_ref[span_of(c), :] = mm(high, b_ref[span_of(c), :]) + mm(low, b_ref[span_of(c), :])

    ends = [lanes(cum_ref[:, (c + 1) * CHUNK - 1:(c + 1) * CHUNK]) for c in range(chunks)]
    before = [jnp.zeros_like(ends[0])]
    for end in ends:
        before.append(before[-1] + end)
    after = [jnp.zeros_like(ends[0])]
    for end in reversed(ends):
        after.insert(0, after[0] + end)
    skip = lanes(knob_ref[:, 2:3])
    rate = lanes(knob_ref[:, 1:2])
    rows, cols, crossed = [], [], None
    for c in range(chunks):
        at = span_of(c)
        cum, dt = cum_ref[:, at], dt_ref[:, at]
        reach = jnp.exp(cum)
        weight = jnp.exp(ends[c] - cum) * dt
        state = per_head(jnp.exp(before[c]), sin_ref[...])
        if c > 0:
            state = state + s_ref[c - 1]
        back = per_head(jnp.exp(after[c + 1]), rin_ref[...])
        if c < chunks - 1:
            back = back + r_ref[c + 1]
        s_high, s_low = split(state)
        r_high, r_low = split(back)
        b, cc = b_ref[at, :], c_ref[at, :]
        xt, gt = xt_ref[:, at].astype(F32), gt_ref[:, at].astype(F32)
        y = mm_nt(s_high, cc) + mm_nt(s_low, cc)
        rows.append(row_ref[:, at] + head_sums(y * gt, heads) * reach)
        dx = per_head(weight, mm_nt(r_high, b) + mm_nt(r_low, b))
        cols.append(col_ref[:, at] + head_sums(dx * xt, heads))
        product = head_sums(xt * gt, heads)
        crossed = product if crossed is None else crossed + product
        dx = dx + dxt_ref[:, at] + per_head(skip, gt)
        gx_ref[at, :] = dx.astype(BF16).T
        reach_t, weight_t = reach.T, weight.T
        dc = jnp.zeros((CHUNK, cc.shape[1]), F32)
        db = jnp.zeros((CHUNK, cc.shape[1]), F32)
        width = cc.shape[1]
        for pair in range(heads // 2):
            wide = slice(pair * 2 * size, (pair + 1) * 2 * size)
            one = slice(2 * pair * size, (2 * pair + 1) * size)
            two = slice((2 * pair + 1) * size, (2 * pair + 2) * size)
            g_pair, x_pair = g_ref[at, wide], x_ref[at, wide]
            gs = (mm(g_pair, pair_blocks(s_high[one], s_high[two]))
                  + mm(g_pair, pair_blocks(s_low[one], s_low[two])))
            xr = (mm(x_pair, pair_blocks(r_high[one], r_high[two]))
                  + mm(x_pair, pair_blocks(r_low[one], r_low[two])))
            for j in range(2):
                h = 2 * pair + j
                dc = dc + gs[:, j * width:(j + 1) * width] * reach_t[:, h:h + 1]
                db = db + xr[:, j * width:(j + 1) * width] * weight_t[:, h:h + 1]
        dc_ref[at, :] += dc
        db_ref[at, :] += db
    last = s_ref[chunks - 1] + per_head(jnp.exp(before[chunks]), sin_ref[...])
    beyond = lanes(jnp.sum(head_sums(last * rin_ref[...], heads), axis=1, keepdims=True))
    suffix = triangle(True).astype(F32)
    g_rate = jnp.zeros((heads, 1), F32)
    g_bias = jnp.zeros((heads, 1), F32)
    for c in reversed(range(chunks)):
        at = span_of(c)
        change = rows[c] - cols[c]
        d_log = jnp.dot(change, suffix, precision=HIGH) + beyond
        beyond = beyond + lanes(jnp.sum(change, axis=1, keepdims=True))
        dt = dt_ref[:, at]
        g_dt = cols[c] / dt - rate * d_log
        v = raw_ref[:, at] + knob_ref[:, 0:1]
        g_raw = g_dt / (1.0 + jnp.exp(-v))
        graw_ref[:, at] = g_raw
        g_rate = g_rate - jnp.sum(dt * d_log, axis=1, keepdims=True)
        g_bias = g_bias + jnp.sum(g_raw, axis=1, keepdims=True)
    g_skip = jnp.sum(crossed, axis=1, keepdims=True)
    lane = lax.broadcasted_iota(jnp.int32, (heads, CHUNK), 1)
    gparam_ref[...] = jnp.where(lane == 0, g_rate, jnp.where(lane == 1, g_skip, g_bias))


def hypercube_shift(value, axis, distance):
    peers = lax.axis_size(axis)
    return lax.ppermute(value, axis, [(i, i ^ distance) for i in range(peers)])


def carried(span, states, adjoints, axis):
    peers, place = lax.axis_size(axis), lax.axis_index(axis)
    heads = span.shape[0]
    half = heads // 2
    odd = (place % 2) == 1

    def halves(whole):
        first, second = whole[:half], whole[half:]
        return jnp.where(odd, second, first), jnp.where(odd, first, second)

    def scale(log):
        return jnp.exp(log)[:, None, None]

    s_mine, s_theirs = halves(states)
    r_mine, r_theirs = halves(adjoints)
    other = hypercube_shift(span, axis, 1)
    s_got, r_got = hypercube_shift((s_theirs, r_theirs), axis, 1)
    log_mine, log_got = halves(span)[0], halves(other)[0]
    log_even, log_odd = jnp.where(odd, log_got, log_mine), jnp.where(odd, log_mine, log_got)
    s_even, s_odd = jnp.where(odd, s_got, s_mine), jnp.where(odd, s_mine, s_got)
    r_even, r_odd = jnp.where(odd, r_got, r_mine), jnp.where(odd, r_mine, r_got)
    s_all = scale(log_odd) * s_even + s_odd
    r_all = r_even + scale(log_even) * r_odd
    log_all = log_even + log_odd
    s_pre, r_pre = jnp.zeros_like(s_all), jnp.zeros_like(r_all)
    s_log, r_log = jnp.zeros_like(log_all), jnp.zeros_like(log_all)
    distance = 2
    while distance < peers:
        upper = (place // distance) % 2 == 1
        final = distance * 2 >= peers
        log_new = hypercube_shift(log_all, axis, distance)
        if final:
            s_new = r_new = hypercube_shift(jnp.where(upper, r_all, s_all), axis, distance)
        else:
            s_new = hypercube_shift(s_all, axis, distance)
            r_new = hypercube_shift(r_all, axis, distance)
        s_pre = jnp.where(upper, s_pre + scale(s_log) * s_new, s_pre)
        r_pre = jnp.where(upper, r_pre, r_pre + scale(r_log) * r_new)
        if not final:
            s_log = jnp.where(upper, s_log + log_new, s_log)
            r_log = jnp.where(upper, r_log, r_log + log_new)
            s_all = jnp.where(upper, scale(log_all) * s_new + s_all, scale(log_new) * s_all + s_new)
            r_all = jnp.where(upper, r_new + scale(log_new) * r_all, r_all + scale(log_all) * r_new)
            log_all = log_all + log_new
        distance *= 2
    s_for_odd = s_even + scale(log_even) * s_pre
    r_for_even = r_odd + scale(log_odd) * r_pre
    s_keep, s_give = jnp.where(odd, s_for_odd, s_pre), jnp.where(odd, s_pre, s_for_odd)
    r_keep, r_give = jnp.where(odd, r_pre, r_for_even), jnp.where(odd, r_for_even, r_pre)
    s_back, r_back = hypercube_shift((s_give, r_give), axis, 1)

    def whole(keep, back):
        return jnp.concatenate([jnp.where(odd, back, keep), jnp.where(odd, keep, back)], axis=0)

    return whole(s_keep, s_back), whole(r_keep, r_back)


def reduce_over(value, axis):
    peers, place = lax.axis_size(axis), lax.axis_index(axis)
    rows = value.shape[1] // peers

    def shift(piece, step):
        return lax.ppermute(piece, axis, [(i, (i + step) % peers) for i in range(peers)])

    def piece_of(owner):
        return lax.dynamic_slice_in_dim(value, owner * rows, rows, axis=1)

    got = [shift(piece_of((place + step) % peers), step) for step in range(1, peers)]
    total = piece_of(place)
    for piece in got:
        total = total + piece
    every = jnp.stack([total] + [shift(total, step) for step in range(1, peers)])
    ordered = [every[(place - owner) % peers] for owner in range(peers)]
    return [jnp.concatenate([piece[k] for piece in ordered], axis=0) for k in range(2)]


def on_device(tokens_x, raw_dt, in_b, in_c, decay_rate, skip_gain, step_bias, grad_y):
    heads, tokens = raw_dt.shape
    width = tokens_x.shape[1]
    size = width // heads
    state = in_b.shape[1]
    chunks = tokens // CHUNK
    wide = GROUP * size
    grid = (heads // GROUP,)

    def shape(*dims, dtype=F32):
        return jax.ShapeDtypeStruct(dims, dtype)

    tokens_by_wide = pl.BlockSpec((tokens, wide), lambda i: (0, i))
    wide_by_tokens = pl.BlockSpec((wide, tokens), lambda i: (i, 0))
    head_rows = pl.BlockSpec((GROUP, tokens), lambda i: (i, 0))
    head_lanes = pl.BlockSpec((GROUP, CHUNK), lambda i: (i, 0))
    head_knobs = pl.BlockSpec((GROUP, 3), lambda i: (i, 0))
    projection = pl.BlockSpec((tokens, state), lambda i: (0, 0))
    state_block = pl.BlockSpec((wide, state), lambda i: (i, 0))
    state_blocks = pl.BlockSpec((chunks, wide, state), lambda i: (0, i, 0))
    projections = pl.BlockSpec((2, tokens, state), lambda i: (0, 0, 0))
    score_blocks = pl.BlockSpec((chunks, CHUNK, CHUNK), lambda i: (0, 0, 0))
    knobs = jnp.stack([step_bias, decay_rate, skip_gain], axis=1)

    xt, gt, dt, cum, end, s_loc, r_loc = pl.pallas_call(
        states_kernel,
        grid=grid,
        in_specs=[tokens_by_wide, tokens_by_wide, head_rows, head_knobs,
                  projection, projection],
        out_specs=[wide_by_tokens, wide_by_tokens, head_rows, head_rows, head_lanes,
                   state_blocks, state_blocks],
        out_shape=[shape(width, tokens, dtype=BF16), shape(width, tokens, dtype=BF16),
                   shape(heads, tokens), shape(heads, tokens), shape(heads, CHUNK),
                   shape(chunks, width, state), shape(chunks, width, state)],
        compiler_params=PARAMS,
        name="states",
    )(tokens_x, grad_y, raw_dt, knobs, in_b, in_c)

    s_in, r_in = carried(
        end[:, 0],
        s_loc[chunks - 1].reshape(heads, size, state),
        r_loc[0].reshape(heads, size, state),
        "ctx",
    )

    dxt, row, col, dg = pl.pallas_call(
        within_kernel,
        grid=grid,
        in_specs=[tokens_by_wide, wide_by_tokens, wide_by_tokens, head_rows, head_rows,
                  projection, projection],
        out_specs=[wide_by_tokens, head_rows, head_rows, score_blocks],
        out_shape=[shape(width, tokens), shape(heads, tokens), shape(heads, tokens),
                   shape(chunks, CHUNK, CHUNK)],
        compiler_params=PARAMS,
        cost_estimate=pl.CostEstimate(
            flops=24 * width * tokens * CHUNK,
            bytes_accessed=14 * width * tokens,
            transcendentals=heads * tokens * CHUNK,
        ),
        name="within",
    )(tokens_x, xt, gt, dt, cum, in_b, in_c)

    grad_x, grad_raw, params, grad_bc = pl.pallas_call(
        across_kernel,
        grid=grid,
        in_specs=[tokens_by_wide, tokens_by_wide, wide_by_tokens, wide_by_tokens, head_rows,
                  head_knobs, head_rows, head_rows, state_blocks,
                  state_blocks, state_block, state_block, wide_by_tokens, head_rows, head_rows,
                  projection, projection, score_blocks],
        out_specs=[tokens_by_wide, head_rows, head_lanes, projections],
        out_shape=[shape(tokens, width, dtype=BF16), shape(heads, tokens), shape(heads, CHUNK),
                   shape(2, tokens, state)],
        compiler_params=PARAMS,
        name="across",
    )(tokens_x, grad_y, xt, gt, raw_dt, knobs, dt, cum, s_loc, r_loc,
      s_in.reshape(width, state), r_in.reshape(width, state), dxt, row, col, in_b, in_c, dg)

    grad_b, grad_c = reduce_over(grad_bc, "head")
    params = params[:, :3]
    distance = 1
    while distance < lax.axis_size("ctx"):
        params = params + hypercube_shift(params, "ctx", distance)
        distance *= 2
    return (grad_x, grad_raw, grad_b, grad_c, params[:, 0], params[:, 1], params[:, 2])


def solution(mesh):
    placed = (
        P("ctx", "head"),
        P("head", "ctx"),
        P("ctx", None),
        P("ctx", None),
        P("head"),
        P("head"),
        P("head"),
        P("ctx", "head"),
    )
    return jax.shard_map(
        on_device,
        mesh=mesh,
        in_specs=placed,
        out_specs=(
            P("ctx", "head"),
            P("head", "ctx"),
            P("ctx", None),
            P("ctx", None),
            P("head"),
            P("head"),
            P("head"),
        ),
        check_vma=False,
    )
```

```python
import jax
import jax.numpy as jnp
from jax import lax
from jax.experimental import pallas as pl
from jax.experimental.pallas import tpu as pltpu
from jax.sharding import PartitionSpec as P


CHUNK = 128
GROUP = 8
F32 = jnp.float32
BF16 = jnp.bfloat16
HIGH = lax.Precision.HIGHEST
NT = (((1,), (1,)), ((), ()))
PARAMS = pltpu.CompilerParams(vmem_limit_bytes=56 << 20)


def mm(a, b):
    return jnp.dot(a, b, preferred_element_type=F32)


def mm_nt(a, b):
    return lax.dot_general(a, b, NT, preferred_element_type=F32)


def split(a):
    high = a.astype(BF16)
    return high, (a - high.astype(F32)).astype(BF16)


def softplus(v):
    return jnp.maximum(v, 0.0) + jnp.log1p(jnp.exp(-jnp.abs(v)))


def lanes(column, width=CHUNK):
    return jnp.broadcast_to(column, (column.shape[0], width))


def per_head(rows, matrix):
    heads = rows.shape[0]
    shaped = matrix.reshape(heads, matrix.shape[0] // heads, matrix.shape[1])
    return (shaped * rows[:, None, :]).reshape(matrix.shape)


def head_sums(matrix, heads):
    return jnp.sum(matrix.reshape(heads, matrix.shape[0] // heads, matrix.shape[1]), axis=1)


def pair_blocks(first, second):
    zero = jnp.zeros_like(first)
    return jnp.concatenate(
        [jnp.concatenate([first, zero], axis=1), jnp.concatenate([zero, second], axis=1)], axis=0
    )


def triangle(lower):
    row = lax.broadcasted_iota(jnp.int32, (CHUNK, CHUNK), 0)
    col = lax.broadcasted_iota(jnp.int32, (CHUNK, CHUNK), 1)
    return (row >= col) if lower else (row <= col)


def span_of(c):
    return slice(c * CHUNK, (c + 1) * CHUNK)


def states_kernel(odd_ref, x_ref, g_ref, raw_ref, knob_ref, b_ref, c_ref,
                  xt_ref, gt_ref, dt_ref, cum_ref, end_ref, s_ref, r_ref,
                  s_mine_ref, s_theirs_ref, r_mine_ref, r_theirs_ref):
    heads, tokens = raw_ref.shape
    chunks = tokens // CHUNK
    dt = softplus(raw_ref[...] + knob_ref[:, 0:1])
    dt_ref[...] = dt
    log_decay = -knob_ref[:, 1:2] * dt
    ones = triangle(False).astype(F32)
    xt_ref[...] = x_ref[...].T
    gt_ref[...] = g_ref[...].T
    cums = [jnp.dot(log_decay[:, span_of(c)], ones, precision=HIGH) for c in range(chunks)]
    ends = [lanes(cum[:, CHUNK - 1:]) for cum in cums]
    total = ends[0]
    for end in ends[1:]:
        total = total + end
    end_ref[...] = total
    state = None
    for c in range(chunks):
        cum_ref[:, span_of(c)] = cums[c]
        weight = jnp.exp(ends[c] - cums[c]) * dt[:, span_of(c)]
        high, low = split(per_head(weight, xt_ref[:, span_of(c)].astype(F32)))
        b = b_ref[span_of(c), :]
        added = mm(high, b) + mm(low, b)
        state = added if state is None else per_head(jnp.exp(ends[c]), state) + added
        s_ref[c] = state
    back = None
    for c in reversed(range(chunks)):
        high, low = split(per_head(jnp.exp(cums[c]), gt_ref[:, span_of(c)].astype(F32)))
        cc = c_ref[span_of(c), :]
        added = mm(high, cc) + mm(low, cc)
        back = added if back is None else per_head(jnp.exp(ends[c]), back) + added
        r_ref[c] = back
    for value, mine, theirs in ((state, s_mine_ref, s_theirs_ref), (back, r_mine_ref, r_theirs_ref)):
        shaped = value.reshape(heads, value.shape[0] // heads, value.shape[1])
        half = shaped.shape[1] // 2
        first, second = shaped[:, :half], shaped[:, half:]

        @pl.when(odd_ref[0] == 0)
        def _():
            mine[...] = first
            theirs[...] = second

        @pl.when(odd_ref[0] == 1)
        def _():
            mine[...] = second
            theirs[...] = first


def within_kernel(x_ref, xt_ref, gt_ref, dt_ref, cum_ref, b_ref, c_ref,
                  dxt_ref, row_ref, col_ref, dg_ref):
    heads, tokens = dt_ref.shape
    size = xt_ref.shape[0] // heads
    group = pl.program_id(0)
    causal = triangle(False)

    @pl.when(group == 0)
    def _():
        dg_ref[...] = jnp.zeros_like(dg_ref)

    def one_chunk(c, carry):
        at = pl.ds(pl.multiple_of(c * CHUNK, CHUNK), CHUNK)
        scores = mm_nt(b_ref[at, :], c_ref[at, :])
        cum = cum_ref[:, at]
        shifted = (cum - jnp.log(dt_ref[:, at])).T
        total = jnp.zeros((CHUNK, CHUNK), F32)
        rows, cols = [], []
        for pair in range(heads // 2):
            x_pair = x_ref[at, pair * 2 * size:(pair + 1) * 2 * size]
            places = [slice((2 * pair + j) * size, (2 * pair + j + 1) * size) for j in range(2)]
            products = mm(x_pair, pair_blocks(gt_ref[places[0], at], gt_ref[places[1], at]))
            for j in range(2):
                h = 2 * pair + j
                gap = cum[h:h + 1, :] - shifted[:, h:h + 1]
                decay = jnp.exp(jnp.where(causal, gap, -1e30))
                total = total + products[:, j * CHUNK:(j + 1) * CHUNK] * decay
                high, low = split(decay * scores)
                x_h = xt_ref[places[j], at]
                g_h = gt_ref[places[j], at]
                y_h = mm(x_h, high) + mm(x_h, low)
                dx_h = mm_nt(g_h, high) + mm_nt(g_h, low)
                dxt_ref[places[j], at] = dx_h
                rows.append(jnp.sum(y_h * g_h.astype(F32), axis=0, keepdims=True))
                cols.append(jnp.sum(dx_h * x_h.astype(F32), axis=0, keepdims=True))
        row_ref[:, at] = jnp.concatenate(rows, axis=0)
        col_ref[:, at] = jnp.concatenate(cols, axis=0)
        dg_ref[c] += total
        return carry

    lax.fori_loop(0, tokens // CHUNK, one_chunk, 0)


def across_kernel(odd_ref, x_ref, g_ref, xt_ref, gt_ref, raw_ref, knob_ref, dt_ref, cum_ref,
                  s_ref, r_ref, s_keep_ref, s_back_ref, r_keep_ref, r_back_ref,
                  dxt_ref, row_ref, col_ref,
                  b_ref, c_ref, dg_ref,
                  gx_ref, graw_ref, gparam_ref, dbc_ref, in_ref):
    db_ref, dc_ref = dbc_ref.at[0], dbc_ref.at[1]
    heads, tokens = dt_ref.shape
    chunks = tokens // CHUNK
    size = xt_ref.shape[0] // heads
    group = pl.program_id(0)

    @pl.when(group == 0)
    def _():
        for c in range(chunks):
            high, low = split(dg_ref[c])
            db_ref[span_of(c), :] = mm(high, c_ref[span_of(c), :]) + mm(low, c_ref[span_of(c), :])
            high, low = split(dg_ref[c].T)
            dc_ref[span_of(c), :] = mm(high, b_ref[span_of(c), :]) + mm(low, b_ref[span_of(c), :])

    half = size // 2
    for k, (keep, given) in enumerate(((s_keep_ref, s_back_ref), (r_keep_ref, r_back_ref))):

        @pl.when(odd_ref[0] == 0)
        def _():
            in_ref[k, :, :half, :] = keep[...]
            in_ref[k, :, half:, :] = given[...]

        @pl.when(odd_ref[0] == 1)
        def _():
            in_ref[k, :, :half, :] = given[...]
            in_ref[k, :, half:, :] = keep[...]

    s_in = in_ref[0].reshape(xt_ref.shape[0], b_ref.shape[1])
    r_in = in_ref[1].reshape(xt_ref.shape[0], b_ref.shape[1])
    ends = [lanes(cum_ref[:, (c + 1) * CHUNK - 1:(c + 1) * CHUNK]) for c in range(chunks)]
    before = [jnp.zeros_like(ends[0])]
    for end in ends:
        before.append(before[-1] + end)
    after = [jnp.zeros_like(ends[0])]
    for end in reversed(ends):
        after.insert(0, after[0] + end)
    skip = lanes(knob_ref[:, 2:3])
    rate = lanes(knob_ref[:, 1:2])
    rows, cols, crossed = [], [], None
    for c in range(chunks):
        at = span_of(c)
        cum, dt = cum_ref[:, at], dt_ref[:, at]
        reach = jnp.exp(cum)
        weight = jnp.exp(ends[c] - cum) * dt
        state = per_head(jnp.exp(before[c]), s_in)
        if c > 0:
            state = state + s_ref[c - 1]
        back = per_head(jnp.exp(after[c + 1]), r_in)
        if c < chunks - 1:
            back = back + r_ref[c + 1]
        s_high, s_low = split(state)
        r_high, r_low = split(back)
        b, cc = b_ref[at, :], c_ref[at, :]
        xt, gt = xt_ref[:, at].astype(F32), gt_ref[:, at].astype(F32)
        y = mm_nt(s_high, cc) + mm_nt(s_low, cc)
        rows.append(row_ref[:, at] + head_sums(y * gt, heads) * reach)
        dx = per_head(weight, mm_nt(r_high, b) + mm_nt(r_low, b))
        cols.append(col_ref[:, at] + head_sums(dx * xt, heads))
        product = head_sums(xt * gt, heads)
        crossed = product if crossed is None else crossed + product
        dx = dx + dxt_ref[:, at] + per_head(skip, gt)
        gx_ref[at, :] = dx.astype(BF16).T
        reach_t, weight_t = reach.T, weight.T
        dc = jnp.zeros((CHUNK, cc.shape[1]), F32)
        db = jnp.zeros((CHUNK, cc.shape[1]), F32)
        width = cc.shape[1]
        for pair in range(heads // 2):
            wide = slice(pair * 2 * size, (pair + 1) * 2 * size)
            one = slice(2 * pair * size, (2 * pair + 1) * size)
            two = slice((2 * pair + 1) * size, (2 * pair + 2) * size)
            g_pair, x_pair = g_ref[at, wide], x_ref[at, wide]
            gs = (mm(g_pair, pair_blocks(s_high[one], s_high[two]))
                  + mm(g_pair, pair_blocks(s_low[one], s_low[two])))
            xr = (mm(x_pair, pair_blocks(r_high[one], r_high[two]))
                  + mm(x_pair, pair_blocks(r_low[one], r_low[two])))
            for j in range(2):
                h = 2 * pair + j
                dc = dc + gs[:, j * width:(j + 1) * width] * reach_t[:, h:h + 1]
                db = db + xr[:, j * width:(j + 1) * width] * weight_t[:, h:h + 1]
        dc_ref[at, :] += dc
        db_ref[at, :] += db
    last = s_ref[chunks - 1] + per_head(jnp.exp(before[chunks]), s_in)
    beyond = lanes(jnp.sum(head_sums(last * r_in, heads), axis=1, keepdims=True))
    suffix = triangle(True).astype(F32)
    g_rate = jnp.zeros((heads, 1), F32)
    g_bias = jnp.zeros((heads, 1), F32)
    for c in reversed(range(chunks)):
        at = span_of(c)
        change = rows[c] - cols[c]
        d_log = jnp.dot(change, suffix, precision=HIGH) + beyond
        beyond = beyond + lanes(jnp.sum(change, axis=1, keepdims=True))
        dt = dt_ref[:, at]
        g_dt = cols[c] / dt - rate * d_log
        v = raw_ref[:, at] + knob_ref[:, 0:1]
        g_raw = g_dt / (1.0 + jnp.exp(-v))
        graw_ref[:, at] = g_raw
        g_rate = g_rate - jnp.sum(dt * d_log, axis=1, keepdims=True)
        g_bias = g_bias + jnp.sum(g_raw, axis=1, keepdims=True)
    g_skip = jnp.sum(crossed, axis=1, keepdims=True)
    lane = lax.broadcasted_iota(jnp.int32, (heads, CHUNK), 1)
    gparam_ref[...] = jnp.where(lane == 0, g_rate, jnp.where(lane == 1, g_skip, g_bias))


def hypercube_shift(value, axis, distance):
    peers = lax.axis_size(axis)
    return lax.ppermute(value, axis, [(i, i ^ distance) for i in range(peers)])


def carried(span, states, adjoints, axis):
    peers, place = lax.axis_size(axis), lax.axis_index(axis)
    odd = (place % 2) == 1
    (s_mine, s_theirs), (r_mine, r_theirs) = states, adjoints

    def scale(log):
        return jnp.exp(log)[:, None, None]

    other = hypercube_shift(span, axis, 1)
    s_got, r_got = hypercube_shift((s_theirs, r_theirs), axis, 1)
    log_even, log_odd = jnp.where(odd, other, span), jnp.where(odd, span, other)
    s_even, s_odd = jnp.where(odd, s_got, s_mine), jnp.where(odd, s_mine, s_got)
    r_even, r_odd = jnp.where(odd, r_got, r_mine), jnp.where(odd, r_mine, r_got)
    s_all = scale(log_odd) * s_even + s_odd
    r_all = r_even + scale(log_even) * r_odd
    log_all = log_even + log_odd
    s_pre, r_pre = jnp.zeros_like(s_all), jnp.zeros_like(r_all)
    s_log, r_log = jnp.zeros_like(log_all), jnp.zeros_like(log_all)
    distance = 2
    while distance < peers:
        upper = (place // distance) % 2 == 1
        final = distance * 2 >= peers
        log_new = hypercube_shift(log_all, axis, distance)
        if final:
            s_new = r_new = hypercube_shift(jnp.where(upper, r_all, s_all), axis, distance)
        else:
            s_new = hypercube_shift(s_all, axis, distance)
            r_new = hypercube_shift(r_all, axis, distance)
        s_pre = jnp.where(upper, s_pre + scale(s_log) * s_new, s_pre)
        r_pre = jnp.where(upper, r_pre, r_pre + scale(r_log) * r_new)
        if not final:
            s_log = jnp.where(upper, s_log + log_new, s_log)
            r_log = jnp.where(upper, r_log, r_log + log_new)
            s_all = jnp.where(upper, scale(log_all) * s_new + s_all, scale(log_new) * s_all + s_new)
            r_all = jnp.where(upper, r_new + scale(log_new) * r_all, r_all + scale(log_all) * r_new)
            log_all = log_all + log_new
        distance *= 2
    s_for_odd = s_even + scale(log_even) * s_pre
    r_for_even = r_odd + scale(log_odd) * r_pre
    s_keep, s_give = jnp.where(odd, s_for_odd, s_pre), jnp.where(odd, s_pre, s_for_odd)
    r_keep, r_give = jnp.where(odd, r_pre, r_for_even), jnp.where(odd, r_for_even, r_pre)
    s_back, r_back = hypercube_shift((s_give, r_give), axis, 1)
    return s_keep, s_back, r_keep, r_back


def reduce_over(value, axis):
    peers, place = lax.axis_size(axis), lax.axis_index(axis)
    rows = value.shape[1] // peers

    def shift(piece, step):
        return lax.ppermute(piece, axis, [(i, (i + step) % peers) for i in range(peers)])

    def piece_of(owner):
        return lax.dynamic_slice_in_dim(value, owner * rows, rows, axis=1)

    got = []
    for step in range(1, peers):
        got.append(shift(piece_of((place + step) % peers), step))
    total = piece_of(place)
    for piece in got:
        total = total + piece
    every = [total]
    for step in range(1, peers):
        every.append(shift(total, step))
    every = jnp.stack(every)
    ordered = [every[(place - owner) % peers] for owner in range(peers)]
    return [jnp.concatenate([piece[k] for piece in ordered], axis=0) for k in range(2)]


def on_device(tokens_x, raw_dt, in_b, in_c, decay_rate, skip_gain, step_bias, grad_y):
    heads, tokens = raw_dt.shape
    width = tokens_x.shape[1]
    size = width // heads
    state = in_b.shape[1]
    chunks = tokens // CHUNK
    wide = GROUP * size
    grid = (heads // GROUP,)

    def shape(*dims, dtype=F32):
        return jax.ShapeDtypeStruct(dims, dtype)

    tokens_by_wide = pl.BlockSpec((tokens, wide), lambda i: (0, i))
    wide_by_tokens = pl.BlockSpec((wide, tokens), lambda i: (i, 0))
    head_rows = pl.BlockSpec((GROUP, tokens), lambda i: (i, 0))
    head_lanes = pl.BlockSpec((GROUP, CHUNK), lambda i: (i, 0))
    head_knobs = pl.BlockSpec((GROUP, 3), lambda i: (i, 0))
    projection = pl.BlockSpec((tokens, state), lambda i: (0, 0))
    half_block = pl.BlockSpec((GROUP, size // 2, state), lambda i: (i, 0, 0))
    half_shape = shape(heads, size // 2, state)
    scalar = pl.BlockSpec(memory_space=pltpu.SMEM)
    odd = (lax.axis_index("ctx") % 2).astype(jnp.int32).reshape(1)
    state_blocks = pl.BlockSpec((chunks, wide, state), lambda i: (0, i, 0))
    projections = pl.BlockSpec((2, tokens, state), lambda i: (0, 0, 0))
    score_blocks = pl.BlockSpec((chunks, CHUNK, CHUNK), lambda i: (0, 0, 0))
    knobs = jnp.stack([step_bias, decay_rate, skip_gain], axis=1)

    xt, gt, dt, cum, end, s_loc, r_loc, *halves = pl.pallas_call(
        states_kernel,
        grid=grid,
        in_specs=[scalar, tokens_by_wide, tokens_by_wide, head_rows, head_knobs,
                  projection, projection],
        out_specs=[wide_by_tokens, wide_by_tokens, head_rows, head_rows, head_lanes,
                   state_blocks, state_blocks] + [half_block] * 4,
        out_shape=[shape(width, tokens, dtype=BF16), shape(width, tokens, dtype=BF16),
                   shape(heads, tokens), shape(heads, tokens), shape(heads, CHUNK),
                   shape(chunks, width, state), shape(chunks, width, state)] + [half_shape] * 4,
        compiler_params=PARAMS,
        name="states",
    )(odd, tokens_x, grad_y, raw_dt, knobs, in_b, in_c)

    arrived = carried(end[:, 0], halves[:2], halves[2:], "ctx")

    dxt, row, col, dg = pl.pallas_call(
        within_kernel,
        grid=grid,
        in_specs=[tokens_by_wide, wide_by_tokens, wide_by_tokens, head_rows, head_rows,
                  projection, projection],
        out_specs=[wide_by_tokens, head_rows, head_rows, score_blocks],
        out_shape=[shape(width, tokens), shape(heads, tokens), shape(heads, tokens),
                   shape(chunks, CHUNK, CHUNK)],
        compiler_params=PARAMS,
        cost_estimate=pl.CostEstimate(
            flops=24 * width * tokens * CHUNK,
            bytes_accessed=14 * width * tokens,
            transcendentals=heads * tokens * CHUNK,
        ),
        name="within",
    )(tokens_x, xt, gt, dt, cum, in_b, in_c)

    grad_x, grad_raw, params, grad_bc = pl.pallas_call(
        across_kernel,
        grid=grid,
        in_specs=[scalar, tokens_by_wide, tokens_by_wide, wide_by_tokens, wide_by_tokens, head_rows,
                  head_knobs, head_rows, head_rows, state_blocks,
                  state_blocks, half_block, half_block, half_block, half_block, wide_by_tokens, head_rows, head_rows,
                  projection, projection, score_blocks],
        out_specs=[tokens_by_wide, head_rows, head_lanes, projections],
        out_shape=[shape(tokens, width, dtype=BF16), shape(heads, tokens), shape(heads, CHUNK),
                   shape(2, tokens, state)],
        scratch_shapes=[pltpu.VMEM((2, GROUP, size, state), F32)],
        compiler_params=PARAMS,
        name="across",
    )(odd, tokens_x, grad_y, xt, gt, raw_dt, knobs, dt, cum, s_loc, r_loc,
      *arrived, dxt, row, col, in_b, in_c, dg)

    grad_b, grad_c = reduce_over(grad_bc, "head")
    params = params[:, :3]
    distance = 1
    while distance < lax.axis_size("ctx"):
        params = params + hypercube_shift(params, "ctx", distance)
        distance *= 2
    return (grad_x, grad_raw, grad_b, grad_c, params[:, 0], params[:, 1], params[:, 2])


def solution(mesh):
    placed = (
        P("ctx", "head"),
        P("head", "ctx"),
        P("ctx", None),
        P("ctx", None),
        P("head"),
        P("head"),
        P("head"),
        P("ctx", "head"),
    )
    return jax.shard_map(
        on_device,
        mesh=mesh,
        in_specs=placed,
        out_specs=(
            P("ctx", "head"),
            P("head", "ctx"),
            P("ctx", None),
            P("ctx", None),
            P("head"),
            P("head"),
            P("head"),
        ),
        check_vma=False,
    )
```

```python
import jax
import jax.numpy as jnp
from jax import lax
from jax.experimental import pallas as pl
from jax.experimental.pallas import tpu as pltpu
from jax.sharding import PartitionSpec as P


CHUNK = 128
GROUP = 8
F32 = jnp.float32
BF16 = jnp.bfloat16
HIGH = lax.Precision.HIGHEST
NT = (((1,), (1,)), ((), ()))
PARAMS = pltpu.CompilerParams(vmem_limit_bytes=56 << 20)


def mm(a, b):
    return jnp.dot(a, b, preferred_element_type=F32)


def mm_nt(a, b):
    return lax.dot_general(a, b, NT, preferred_element_type=F32)


def split(a):
    high = a.astype(BF16)
    return high, (a - high.astype(F32)).astype(BF16)


def softplus(v):
    return jnp.maximum(v, 0.0) + jnp.log1p(jnp.exp(-jnp.abs(v)))


def lanes(column, width=CHUNK):
    return jnp.broadcast_to(column, (column.shape[0], width))


def per_head(rows, matrix):
    heads = rows.shape[0]
    shaped = matrix.reshape(heads, matrix.shape[0] // heads, matrix.shape[1])
    return (shaped * rows[:, None, :]).reshape(matrix.shape)


def head_sums(matrix, heads):
    return jnp.sum(matrix.reshape(heads, matrix.shape[0] // heads, matrix.shape[1]), axis=1)


def pair_blocks(first, second):
    zero = jnp.zeros_like(first)
    return jnp.concatenate(
        [jnp.concatenate([first, zero], axis=1), jnp.concatenate([zero, second], axis=1)], axis=0
    )


def triangle(lower):
    row = lax.broadcasted_iota(jnp.int32, (CHUNK, CHUNK), 0)
    col = lax.broadcasted_iota(jnp.int32, (CHUNK, CHUNK), 1)
    return (row >= col) if lower else (row <= col)


def span_of(c):
    return slice(c * CHUNK, (c + 1) * CHUNK)


def states_kernel(odd_ref, x_ref, g_ref, raw_ref, knob_ref, b_ref, c_ref,
                  xt_ref, gt_ref, dt_ref, cum_ref, end_ref, s_ref, r_ref,
                  s_mine_ref, s_theirs_ref, r_mine_ref, r_theirs_ref):
    heads, tokens = raw_ref.shape
    chunks = tokens // CHUNK
    dt = softplus(raw_ref[...] + knob_ref[:, 0:1])
    dt_ref[...] = dt
    log_decay = -knob_ref[:, 1:2] * dt
    ones = triangle(False).astype(F32)
    xt_ref[...] = x_ref[...].T
    gt_ref[...] = g_ref[...].T
    cums = [jnp.dot(log_decay[:, span_of(c)], ones, precision=HIGH) for c in range(chunks)]
    ends = [lanes(cum[:, CHUNK - 1:]) for cum in cums]
    total = ends[0]
    for end in ends[1:]:
        total = total + end
    end_ref[...] = total
    state = None
    for c in range(chunks):
        cum_ref[:, span_of(c)] = cums[c]
        weight = jnp.exp(ends[c] - cums[c]) * dt[:, span_of(c)]
        high, low = split(per_head(weight, xt_ref[:, span_of(c)].astype(F32)))
        b = b_ref[span_of(c), :]
        added = mm(high, b) + mm(low, b)
        state = added if state is None else per_head(jnp.exp(ends[c]), state) + added
        s_ref[c] = state
    back = None
    for c in reversed(range(chunks)):
        high, low = split(per_head(jnp.exp(cums[c]), gt_ref[:, span_of(c)].astype(F32)))
        cc = c_ref[span_of(c), :]
        added = mm(high, cc) + mm(low, cc)
        back = added if back is None else per_head(jnp.exp(ends[c]), back) + added
        r_ref[c] = back
    for value, mine, theirs in ((state, s_mine_ref, s_theirs_ref), (back, r_mine_ref, r_theirs_ref)):
        shaped = value.reshape(heads, value.shape[0] // heads, value.shape[1])
        half = shaped.shape[1] // 2
        first, second = shaped[:, :half], shaped[:, half:]

        @pl.when(odd_ref[0] == 0)
        def _():
            mine[...] = first
            theirs[...] = second

        @pl.when(odd_ref[0] == 1)
        def _():
            mine[...] = second
            theirs[...] = first


def within_kernel(x_ref, xt_ref, gt_ref, dt_ref, cum_ref, b_ref, c_ref,
                  dxt_ref, row_ref, col_ref, dg_ref):
    heads, tokens = dt_ref.shape
    size = xt_ref.shape[0] // heads
    group = pl.program_id(0)
    causal = triangle(False)

    @pl.when(group == 0)
    def _():
        dg_ref[...] = jnp.zeros_like(dg_ref)

    def one_chunk(c, carry):
        at = pl.ds(pl.multiple_of(c * CHUNK, CHUNK), CHUNK)
        scores = mm_nt(b_ref[at, :], c_ref[at, :])
        cum = cum_ref[:, at]
        shifted = (cum - jnp.log(dt_ref[:, at])).T
        total = jnp.zeros((CHUNK, CHUNK), F32)
        rows, cols = [], []
        for pair in range(heads // 2):
            x_pair = x_ref[at, pair * 2 * size:(pair + 1) * 2 * size]
            places = [slice((2 * pair + j) * size, (2 * pair + j + 1) * size) for j in range(2)]
            products = mm(x_pair, pair_blocks(gt_ref[places[0], at], gt_ref[places[1], at]))
            for j in range(2):
                h = 2 * pair + j
                gap = cum[h:h + 1, :] - shifted[:, h:h + 1]
                decay = jnp.exp(jnp.where(causal, gap, -1e30))
                total = total + products[:, j * CHUNK:(j + 1) * CHUNK] * decay
                high, low = split(decay * scores)
                x_h = xt_ref[places[j], at]
                g_h = gt_ref[places[j], at]
                y_h = mm(x_h, high) + mm(x_h, low)
                dx_h = mm_nt(g_h, high) + mm_nt(g_h, low)
                dxt_ref[places[j], at] = dx_h
                rows.append(jnp.sum(y_h * g_h.astype(F32), axis=0, keepdims=True))
                cols.append(jnp.sum(dx_h * x_h.astype(F32), axis=0, keepdims=True))
        row_ref[:, at] = jnp.concatenate(rows, axis=0)
        col_ref[:, at] = jnp.concatenate(cols, axis=0)
        dg_ref[c] += total
        return carry

    lax.fori_loop(0, tokens // CHUNK, one_chunk, 0)


def across_kernel(odd_ref, x_ref, g_ref, xt_ref, gt_ref, raw_ref, knob_ref, dt_ref, cum_ref,
                  s_ref, r_ref, s_keep_ref, s_back_ref, r_keep_ref, r_back_ref,
                  dxt_ref, row_ref, col_ref,
                  b_ref, c_ref, dg_ref,
                  gx_ref, graw_ref, gparam_ref, dbc_ref, in_ref):
    db_ref, dc_ref = dbc_ref.at[0], dbc_ref.at[1]
    heads, tokens = dt_ref.shape
    chunks = tokens // CHUNK
    size = xt_ref.shape[0] // heads
    group = pl.program_id(0)

    @pl.when(group == 0)
    def _():
        for c in range(chunks):
            high, low = split(dg_ref[c])
            db_ref[span_of(c), :] = mm(high, c_ref[span_of(c), :]) + mm(low, c_ref[span_of(c), :])
            high, low = split(dg_ref[c].T)
            dc_ref[span_of(c), :] = mm(high, b_ref[span_of(c), :]) + mm(low, b_ref[span_of(c), :])

    half = size // 2
    for k, (keep, given) in enumerate(((s_keep_ref, s_back_ref), (r_keep_ref, r_back_ref))):

        @pl.when(odd_ref[0] == 0)
        def _():
            in_ref[k, :, :half, :] = keep[...]
            in_ref[k, :, half:, :] = given[...]

        @pl.when(odd_ref[0] == 1)
        def _():
            in_ref[k, :, :half, :] = given[...]
            in_ref[k, :, half:, :] = keep[...]

    s_in = in_ref[0].reshape(xt_ref.shape[0], b_ref.shape[1])
    r_in = in_ref[1].reshape(xt_ref.shape[0], b_ref.shape[1])
    ends = [lanes(cum_ref[:, (c + 1) * CHUNK - 1:(c + 1) * CHUNK]) for c in range(chunks)]
    before = [jnp.zeros_like(ends[0])]
    for end in ends:
        before.append(before[-1] + end)
    after = [jnp.zeros_like(ends[0])]
    for end in reversed(ends):
        after.insert(0, after[0] + end)
    skip = lanes(knob_ref[:, 2:3])
    rate = lanes(knob_ref[:, 1:2])
    rows, cols, crossed = [], [], None
    for c in range(chunks):
        at = span_of(c)
        cum, dt = cum_ref[:, at], dt_ref[:, at]
        reach = jnp.exp(cum)
        weight = jnp.exp(ends[c] - cum) * dt
        state = per_head(jnp.exp(before[c]), s_in)
        if c > 0:
            state = state + s_ref[c - 1]
        back = per_head(jnp.exp(after[c + 1]), r_in)
        if c < chunks - 1:
            back = back + r_ref[c + 1]
        s_high, s_low = split(state)
        r_high, r_low = split(back)
        b, cc = b_ref[at, :], c_ref[at, :]
        xt, gt = xt_ref[:, at].astype(F32), gt_ref[:, at].astype(F32)
        y = mm_nt(s_high, cc) + mm_nt(s_low, cc)
        rows.append(row_ref[:, at] + head_sums(y * gt, heads) * reach)
        dx = per_head(weight, mm_nt(r_high, b) + mm_nt(r_low, b))
        cols.append(col_ref[:, at] + head_sums(dx * xt, heads))
        product = head_sums(xt * gt, heads)
        crossed = product if crossed is None else crossed + product
        dx = dx + dxt_ref[:, at] + per_head(skip, gt)
        gx_ref[at, :] = dx.astype(BF16).T
        reach_t, weight_t = reach.T, weight.T
        dc = jnp.zeros((CHUNK, cc.shape[1]), F32)
        db = jnp.zeros((CHUNK, cc.shape[1]), F32)
        width = cc.shape[1]
        for pair in range(heads // 2):
            wide = slice(pair * 2 * size, (pair + 1) * 2 * size)
            one = slice(2 * pair * size, (2 * pair + 1) * size)
            two = slice((2 * pair + 1) * size, (2 * pair + 2) * size)
            g_pair, x_pair = g_ref[at, wide], x_ref[at, wide]
            gs = (mm(g_pair, pair_blocks(s_high[one], s_high[two]))
                  + mm(g_pair, pair_blocks(s_low[one], s_low[two])))
            xr = (mm(x_pair, pair_blocks(r_high[one], r_high[two]))
                  + mm(x_pair, pair_blocks(r_low[one], r_low[two])))
            for j in range(2):
                h = 2 * pair + j
                dc = dc + gs[:, j * width:(j + 1) * width] * reach_t[:, h:h + 1]
                db = db + xr[:, j * width:(j + 1) * width] * weight_t[:, h:h + 1]
        dc_ref[at, :] += dc
        db_ref[at, :] += db
    last = s_ref[chunks - 1] + per_head(jnp.exp(before[chunks]), s_in)
    beyond = lanes(jnp.sum(head_sums(last * r_in, heads), axis=1, keepdims=True))
    suffix = triangle(True).astype(F32)
    g_rate = jnp.zeros((heads, 1), F32)
    g_bias = jnp.zeros((heads, 1), F32)
    for c in reversed(range(chunks)):
        at = span_of(c)
        change = rows[c] - cols[c]
        d_log = jnp.dot(change, suffix, precision=HIGH) + beyond
        beyond = beyond + lanes(jnp.sum(change, axis=1, keepdims=True))
        dt = dt_ref[:, at]
        g_dt = cols[c] / dt - rate * d_log
        v = raw_ref[:, at] + knob_ref[:, 0:1]
        g_raw = g_dt / (1.0 + jnp.exp(-v))
        graw_ref[:, at] = g_raw
        g_rate = g_rate - jnp.sum(dt * d_log, axis=1, keepdims=True)
        g_bias = g_bias + jnp.sum(g_raw, axis=1, keepdims=True)
    g_skip = jnp.sum(crossed, axis=1, keepdims=True)
    lane = lax.broadcasted_iota(jnp.int32, (heads, CHUNK), 1)
    gparam_ref[...] = jnp.where(lane == 0, g_rate, jnp.where(lane == 1, g_skip, g_bias))


def hypercube_shift(value, axis, distance):
    peers = lax.axis_size(axis)
    return lax.ppermute(value, axis, [(i, i ^ distance) for i in range(peers)])


def carried(span, states, adjoints, axis):
    peers, place = lax.axis_size(axis), lax.axis_index(axis)
    odd = (place % 2) == 1
    (s_mine, s_theirs), (r_mine, r_theirs) = states, adjoints

    def scale(log):
        return jnp.exp(log)[:, None, None]

    other = hypercube_shift(span, axis, 1)
    s_got, r_got = hypercube_shift((s_theirs, r_theirs), axis, 1)
    log_even, log_odd = jnp.where(odd, other, span), jnp.where(odd, span, other)
    s_even, s_odd = jnp.where(odd, s_got, s_mine), jnp.where(odd, s_mine, s_got)
    r_even, r_odd = jnp.where(odd, r_got, r_mine), jnp.where(odd, r_mine, r_got)
    s_all = scale(log_odd) * s_even + s_odd
    r_all = r_even + scale(log_even) * r_odd
    log_all = log_even + log_odd
    chips, chip = peers // 2, place // 2

    def onward(value, step):
        return lax.ppermute(value, axis, [(i, (i + 2 * step) % peers) for i in range(peers)])

    got, logs = {}, {}
    for step in range(1, chips):
        logs[step] = onward(log_all, step)
        got[step] = onward(jnp.where(chip + step < chips, s_all, r_all), step)
    s_pre, r_pre = jnp.zeros_like(s_all), jnp.zeros_like(r_all)
    s_log, r_log = jnp.zeros_like(log_all), jnp.zeros_like(log_all)
    for step in range(1, chips):
        back = chips - step
        s_pre = s_pre + jnp.where(chip >= step, scale(s_log), 0.0) * got[step]
        r_pre = r_pre + jnp.where(chip + step < chips, scale(r_log), 0.0) * got[back]
        s_log, r_log = s_log + logs[step], r_log + logs[back]
    s_for_odd = s_even + scale(log_even) * s_pre
    r_for_even = r_odd + scale(log_odd) * r_pre
    s_keep, s_give = jnp.where(odd, s_for_odd, s_pre), jnp.where(odd, s_pre, s_for_odd)
    r_keep, r_give = jnp.where(odd, r_pre, r_for_even), jnp.where(odd, r_for_even, r_pre)
    s_back, r_back = hypercube_shift((s_give, r_give), axis, 1)
    return s_keep, s_back, r_keep, r_back


def reduce_over(value, axis):
    peers, place = lax.axis_size(axis), lax.axis_index(axis)
    rows = value.shape[1] // peers

    def shift(piece, step):
        return lax.ppermute(piece, axis, [(i, (i + step) % peers) for i in range(peers)])

    def piece_of(owner):
        return lax.dynamic_slice_in_dim(value, owner * rows, rows, axis=1)

    got = []
    for step in range(1, peers):
        got.append(shift(piece_of((place + step) % peers), step))
    total = piece_of(place)
    for piece in got:
        total = total + piece
    every = [total]
    for step in range(1, peers):
        every.append(shift(total, step))
    every = jnp.stack(every)
    ordered = [every[(place - owner) % peers] for owner in range(peers)]
    return [jnp.concatenate([piece[k] for piece in ordered], axis=0) for k in range(2)]


def on_device(tokens_x, raw_dt, in_b, in_c, decay_rate, skip_gain, step_bias, grad_y):
    heads, tokens = raw_dt.shape
    width = tokens_x.shape[1]
    size = width // heads
    state = in_b.shape[1]
    chunks = tokens // CHUNK
    wide = GROUP * size
    grid = (heads // GROUP,)

    def shape(*dims, dtype=F32):
        return jax.ShapeDtypeStruct(dims, dtype)

    tokens_by_wide = pl.BlockSpec((tokens, wide), lambda i: (0, i))
    wide_by_tokens = pl.BlockSpec((wide, tokens), lambda i: (i, 0))
    head_rows = pl.BlockSpec((GROUP, tokens), lambda i: (i, 0))
    head_lanes = pl.BlockSpec((GROUP, CHUNK), lambda i: (i, 0))
    head_knobs = pl.BlockSpec((GROUP, 3), lambda i: (i, 0))
    projection = pl.BlockSpec((tokens, state), lambda i: (0, 0))
    half_block = pl.BlockSpec((GROUP, size // 2, state), lambda i: (i, 0, 0))
    half_shape = shape(heads, size // 2, state)
    scalar = pl.BlockSpec(memory_space=pltpu.SMEM)
    odd = (lax.axis_index("ctx") % 2).astype(jnp.int32).reshape(1)
    state_blocks = pl.BlockSpec((chunks, wide, state), lambda i: (0, i, 0))
    projections = pl.BlockSpec((2, tokens, state), lambda i: (0, 0, 0))
    score_blocks = pl.BlockSpec((chunks, CHUNK, CHUNK), lambda i: (0, 0, 0))
    knobs = jnp.stack([step_bias, decay_rate, skip_gain], axis=1)

    xt, gt, dt, cum, end, s_loc, r_loc, *halves = pl.pallas_call(
        states_kernel,
        grid=grid,
        in_specs=[scalar, tokens_by_wide, tokens_by_wide, head_rows, head_knobs,
                  projection, projection],
        out_specs=[wide_by_tokens, wide_by_tokens, head_rows, head_rows, head_lanes,
                   state_blocks, state_blocks] + [half_block] * 4,
        out_shape=[shape(width, tokens, dtype=BF16), shape(width, tokens, dtype=BF16),
                   shape(heads, tokens), shape(heads, tokens), shape(heads, CHUNK),
                   shape(chunks, width, state), shape(chunks, width, state)] + [half_shape] * 4,
        compiler_params=PARAMS,
        name="states",
    )(odd, tokens_x, grad_y, raw_dt, knobs, in_b, in_c)

    arrived = carried(end[:, 0], halves[:2], halves[2:], "ctx")

    dxt, row, col, dg = pl.pallas_call(
        within_kernel,
        grid=grid,
        in_specs=[tokens_by_wide, wide_by_tokens, wide_by_tokens, head_rows, head_rows,
                  projection, projection],
        out_specs=[wide_by_tokens, head_rows, head_rows, score_blocks],
        out_shape=[shape(width, tokens), shape(heads, tokens), shape(heads, tokens),
                   shape(chunks, CHUNK, CHUNK)],
        compiler_params=PARAMS,
        cost_estimate=pl.CostEstimate(
            flops=24 * width * tokens * CHUNK,
            bytes_accessed=14 * width * tokens,
            transcendentals=heads * tokens * CHUNK,
        ),
        name="within",
    )(tokens_x, xt, gt, dt, cum, in_b, in_c)

    grad_x, grad_raw, params, grad_bc = pl.pallas_call(
        across_kernel,
        grid=grid,
        in_specs=[scalar, tokens_by_wide, tokens_by_wide, wide_by_tokens, wide_by_tokens, head_rows,
                  head_knobs, head_rows, head_rows, state_blocks,
                  state_blocks, half_block, half_block, half_block, half_block, wide_by_tokens, head_rows, head_rows,
                  projection, projection, score_blocks],
        out_specs=[tokens_by_wide, head_rows, head_lanes, projections],
        out_shape=[shape(tokens, width, dtype=BF16), shape(heads, tokens), shape(heads, CHUNK),
                   shape(2, tokens, state)],
        scratch_shapes=[pltpu.VMEM((2, GROUP, size, state), F32)],
        compiler_params=PARAMS,
        name="across",
    )(odd, tokens_x, grad_y, xt, gt, raw_dt, knobs, dt, cum, s_loc, r_loc,
      *arrived, dxt, row, col, in_b, in_c, dg)

    grad_b, grad_c = reduce_over(grad_bc, "head")
    params = params[:, :3]
    distance = 1
    while distance < lax.axis_size("ctx"):
        params = params + hypercube_shift(params, "ctx", distance)
        distance *= 2
    return (grad_x, grad_raw, grad_b, grad_c, params[:, 0], params[:, 1], params[:, 2])


def solution(mesh):
    placed = (
        P("ctx", "head"),
        P("head", "ctx"),
        P("ctx", None),
        P("ctx", None),
        P("head"),
        P("head"),
        P("head"),
        P("ctx", "head"),
    )
    return jax.shard_map(
        on_device,
        mesh=mesh,
        in_specs=placed,
        out_specs=(
            P("ctx", "head"),
            P("head", "ctx"),
            P("ctx", None),
            P("ctx", None),
            P("head"),
            P("head"),
            P("head"),
        ),
        check_vma=False,
    )
```
